32 devices in a mesh: obs: 8 (over y, x, core), rows: 4 (over z).
Axes of the slice: x: 2, y: 2, z: 4, core: 2. Of those that a mesh axis runs over, the one named last changes fastest.
Arguments:
- state: float32 [8192, 256], P(('obs', 'rows')), may hold values from -6 to 6
- foot_tiles: int32 [192, 4], P('obs'), may hold values from 0 to 3
- foot_weight: float32 [192, 4, 256], P('obs'), may hold values from -0.25 to 0.25
- azimuth: float32 [768], P('obs'), may hold values from -3.140625 to 3.140625
- obs_value: float32 [768], replicated, may hold values from 0.5 to 2.5
- obs_var: float32 [768], replicated, may hold values from 0.3 to 3
- tile_bin: int32 [32, 768], P(('obs', 'rows')), may hold values from 0 to 14
- obs_bin: int32 [768, 768], P('obs'), may hold values from 0 to 14
- order: int32 [768], replicated, may hold values from 0 to 767, as said below
Outputs:
- analysis: float32 [8192, 256], P(('obs', 'rows'))
The draws below stay inside these ranges and needn't reach their ends.
Inputs may be any that keep to these rules, and one draw needn't show every extreme that they name: foot_tiles numbers a tile among the 4 tiles of the footprint's own observation group. `order`: a permutation of the observables; each aligned block of 128 entries is one batch, and every batch holds equally many observables of each observation group (the 96 observables of group g are g * 96 to g * 96 + 95).
All inputs are finite; a program needn't handle non-finite values.
Results may differ from the reference program's by a relative error of at most 0.0003.
Values sent between devices are 32-bit elements; how exact they have to be, the bound alone decides.
A program may use at most 64 MiB of HBM per device.

```python
import math
import jax
import jax.numpy as jnp
from jax import lax

MEMBERS = 256
BATCH = 128
BATCHES = 6
TILE = 256
FOOT = 4
RADIUS = 8
NROWS = 8192
NTILES = 32
TILES_GRP = 4
NOBS = 768
NFOOT = 192
FOOT_GRP = 24
OBS_GRP = 96


def cycle_bins(key, first_group, second_group, groups):
    apart = jnp.abs(first_group[:, None] - second_group[None, :])
    cycle = jnp.minimum(apart, groups - apart)
    extra = jax.random.randint(key, cycle.shape, 0, 3, dtype=jnp.int32)
    return (3 * cycle + extra).astype(jnp.int32)


def draw_tile_bin(key, part):
    groups = NOBS // OBS_GRP
    tile_group = jnp.arange(NTILES, dtype=jnp.int32) // TILES_GRP
    obs_group = jnp.arange(NOBS, dtype=jnp.int32) // OBS_GRP
    return cycle_bins(jax.random.fold_in(key, 11), tile_group, obs_group, groups)


def draw_obs_bin(key, part):
    groups = NOBS // OBS_GRP
    obs_group = jnp.arange(NOBS, dtype=jnp.int32) // OBS_GRP
    return cycle_bins(jax.random.fold_in(key, 23), obs_group, obs_group, groups)


def draw_order(key, part):
    groups = NOBS // OBS_GRP
    per_batch = OBS_GRP // BATCHES
    group_key, batch_key = jax.random.split(jax.random.fold_in(key, 37))
    within = jax.vmap(lambda single: jax.random.permutation(single, OBS_GRP))(jax.random.split(group_key, groups)).astype(jnp.int32)
    members = within + (jnp.arange(groups, dtype=jnp.int32) * OBS_GRP)[:, None]
    spread = members.reshape(groups, per_batch, BATCHES).transpose(2, 1, 0).reshape(BATCHES, BATCH)
    shuffle = jax.vmap(lambda single: jax.random.permutation(single, BATCH))(jax.random.split(batch_key, BATCHES)).astype(jnp.int32)
    mixed = jnp.take_along_axis(spread, shuffle, axis=1)
    return mixed.reshape(NOBS).astype(jnp.int32)


def plant(array, stream_key, low, largest):
    dims = array.shape
    place = [jax.random.randint(jax.random.fold_in(stream_key, axis), (), 0, dims[axis]) for axis in range(len(dims))]
    array = array.at[tuple(place)].set(low)
    longest = dims.index(max(dims))
    place[longest] = (place[longest] + 1) % dims[longest]
    return array.at[tuple(place)].set(largest)


def level_of(own_key, extent, cuts, least, top_value):
    loudness, own = 1.0, jax.random.fold_in(own_key, 6)
    for dim, blocks in cuts:
        heights = jnp.exp(jax.random.uniform(jax.random.fold_in(own, dim), (blocks,), jnp.float32, least / len(cuts), top_value / len(cuts)))
        loudness = loudness * jnp.repeat(heights, extent[dim] // blocks).reshape([-1 if axis == dim else 1 for axis in range(len(extent))])
    return loudness


def normal_values(stream_key, dims, scale, bound, cuts=(), kind=jnp.bfloat16):
    loudness = level_of(stream_key, dims, cuts, -0.22, 0.18) if cuts else 1.0
    result = jax.random.normal(stream_key, dims, jnp.float32) * scale * loudness
    return jnp.minimum(jnp.maximum(result, -bound), bound).astype(kind)


def setup_inputs(seed: int = 0) -> dict:
    keys = jax.random.split(jax.random.key(seed), 10)
    return {
        "state": normal_values(keys[0], (NROWS, MEMBERS), 1.0, 6.0, ((0, 32),), jnp.float32),
        "foot_tiles": plant(jax.random.randint(keys[1], (NFOOT, FOOT), 0, TILES_GRP), jax.random.fold_in(keys[1], 1), 0, TILES_GRP - 1).astype(jnp.int32),
        "foot_weight": normal_values(keys[2], (NFOOT, FOOT, TILE), (FOOT * TILE // 2) ** -0.5, 0.25, ((0, 8),), jnp.float32),
        "azimuth": jnp.clip(jax.random.uniform(keys[3], (NOBS,), jnp.float32, -3.140625, 3.140625), -3.140625, 3.140625),
        "obs_value": jnp.clip(jax.random.uniform(keys[4], (NOBS,), jnp.float32, 0.5, 2.5), 0.5, 2.5),
        "obs_var": jnp.clip(jnp.exp(jax.random.uniform(keys[5], (NOBS,), jnp.float32, math.log(0.3), math.log(3.0))), 0.3, 3.0),
        "tile_bin": draw_tile_bin(jax.random.fold_in(keys[9], 71), 0),
        "obs_bin": draw_obs_bin(jax.random.fold_in(keys[9], 71), 0),
        "order": draw_order(jax.random.fold_in(keys[9], 71), 0),
    }


HIGH = lax.Precision.HIGHEST

def model_function(east_wind, north_wind, angles):
    speed = jnp.sqrt(east_wind * east_wind + north_wind * north_wind + 1.0)
    cosine = (east_wind * jnp.cos(angles) + north_wind * jnp.sin(angles)) / speed
    return jnp.exp(0.6 * jnp.log(speed)) * (0.7 + 0.4 * cosine + 0.6 * cosine * cosine)

def taper_weight(bins):
    scaled = 1.0 - bins.astype(jnp.float32) / RADIUS
    return jnp.where(bins < RADIUS, scaled * scaled, jnp.zeros_like(scaled))

def batch_gains(batch_obs, values, variances):
    row_mean = lax.optimization_barrier(jnp.mean(batch_obs, axis=1))
    perturb = batch_obs - row_mean[:, None]
    innov = values - row_mean
    covariance = jnp.dot(perturb.astype(jnp.float32), perturb.T.astype(jnp.float32), precision=HIGH, preferred_element_type=jnp.float32) / (MEMBERS - 1) + jnp.diag(variances)
    factor = jnp.linalg.cholesky(covariance)
    middle = jax.scipy.linalg.solve_triangular(factor, innov, lower=True)
    solved = jax.scipy.linalg.solve_triangular(factor, middle, lower=True, trans=1)
    eye_matrix = jnp.eye(BATCH, dtype=jnp.float32)
    shifted = factor + jnp.diag(jnp.sqrt(variances))
    inverse = jax.scipy.linalg.solve_triangular(shifted, eye_matrix, lower=True)
    gain_matrix = jax.scipy.linalg.solve_triangular(factor, inverse, lower=True, trans=1)
    return (perturb, solved, gain_matrix)

def localised(ensemble, weights, rows_per, perturb, solved, gain_matrix):
    row_mean = lax.optimization_barrier(jnp.mean(ensemble, axis=1, keepdims=True))
    deviation = ensemble - row_mean
    product = jnp.dot(deviation.astype(jnp.float32), perturb.T.astype(jnp.float32), precision=HIGH, preferred_element_type=jnp.float32) / (MEMBERS - 1)
    product = (product.reshape(-1, rows_per, BATCH) * weights[:, None, :]).reshape(product.shape)
    row_mean = row_mean + jnp.dot(product.astype(jnp.float32), solved[:, None].astype(jnp.float32), precision=HIGH, preferred_element_type=jnp.float32)
    mixed = jnp.dot(product.astype(jnp.float32), gain_matrix.astype(jnp.float32), precision=HIGH, preferred_element_type=jnp.float32)
    deviation = deviation - jnp.dot(mixed.astype(jnp.float32), perturb.astype(jnp.float32), precision=HIGH, preferred_element_type=jnp.float32)
    return row_mean + deviation

def reference(state, foot_tiles, foot_weight, azimuth, obs_value, obs_var, tile_bin, obs_bin, order):
    half_tile = TILE // 2
    tiles = state.reshape(NTILES, 2, half_tile, MEMBERS)
    group_start = jnp.arange(NFOOT, dtype=jnp.int32) // FOOT_GRP * TILES_GRP
    global_tiles = (foot_tiles + group_start[:, None]).astype(jnp.int32)

    def footprint(inputs):
        listed, weights = inputs
        picked_tiles = tiles[listed]
        return jnp.einsum('thc,thcm->hm', weights.reshape(FOOT, 2, half_tile), picked_tiles, precision=HIGH)
    wind_sums = lax.map(footprint, (global_tiles, foot_weight))
    angles = azimuth.reshape(NFOOT, 4)
    observed = model_function(wind_sums[:, 0, None, :], wind_sums[:, 1, None, :], angles[:, :, None]).reshape(NOBS, MEMBERS)

    def batch_step(carry, batch_num):
        ensemble, observed = carry
        picked = lax.dynamic_slice_in_dim(order, batch_num * BATCH, BATCH).astype(jnp.int32)
        perturb, solved, gain_matrix = batch_gains(observed[picked], obs_value[picked], obs_var[picked])
        ensemble = localised(ensemble, taper_weight(tile_bin[:, picked]), TILE, perturb, solved, gain_matrix)
        observed = localised(observed, taper_weight(obs_bin[:, picked]), 1, perturb, solved, gain_matrix)
        return ((ensemble, observed), None)
    (ensemble, observed), unused = lax.scan(batch_step, (state, observed), jnp.arange(BATCHES, dtype=jnp.int32))
    return ensemble
```

```python
import functools

import jax
import jax.numpy as jnp
from jax import lax
from jax.experimental import pallas as pl
from jax.experimental.pallas import tpu as pltpu
from jax.sharding import PartitionSpec as P

MEMBERS = 256
BATCH = 128
TILE = 256
RADIUS = 8
SUB = 8
F32 = jnp.float32
BF16 = jnp.bfloat16


HIGH = lax.Precision.HIGHEST
VMEM = pl.BlockSpec(memory_space=pltpu.VMEM)


def model_function(east_wind, north_wind, angles):
    speed = jnp.sqrt(east_wind * east_wind + north_wind * north_wind + 1.0)
    cosine = (east_wind * jnp.cos(angles) + north_wind * jnp.sin(angles)) / speed
    return jnp.exp(0.6 * jnp.log(speed)) * (0.7 + 0.4 * cosine + 0.6 * cosine * cosine)


def taper_weight(bins):
    scaled = 1.0 - bins.astype(F32) / RADIUS
    return jnp.where(bins < RADIUS, scaled * scaled, jnp.zeros_like(scaled))


def halves(value):
    high = value.astype(BF16)
    return high, (value - high.astype(F32)).astype(BF16)


def dot3(left, right, dims=(((1,), (0,)), ((), ()))):
    (left_hi, left_lo), (right_hi, right_lo) = left, right
    dot = functools.partial(lax.dot_general, dimension_numbers=dims, preferred_element_type=F32)
    return dot(left_hi, right_hi) + (dot(left_hi, right_lo) + dot(left_lo, right_hi))


NT = (((1,), (1,)), ((), ()))
TN = (((0,), (0,)), ((), ()))


def factor_inverses(covariance, root_row):
    blocks = BATCH // SUB
    lane = lax.broadcasted_iota(jnp.int32, (SUB, BATCH), 1)
    sub = lax.broadcasted_iota(jnp.int32, (SUB, BATCH), 0)
    work = [covariance[SUB * i : SUB * (i + 1), :] for i in range(blocks)]
    second = [(lane == sub + SUB * i).astype(F32) for i in range(blocks)]
    scales = []
    for j in range(BATCH):
        b, s = divmod(j, SUB)
        at_lane = lane == j
        row = jnp.broadcast_to(work[b][s : s + 1, :], (SUB, BATCH))
        pivot = jnp.broadcast_to(work[b][s : s + 1, j : j + 1], (SUB, BATCH))
        inv_root = lax.rsqrt(pivot)
        inv = inv_root * inv_root
        scaled = jnp.where(at_lane, inv, row * inv)
        diag = pivot * inv_root + jnp.broadcast_to(root_row[:, j : j + 1], (SUB, BATCH))
        second_row = jnp.broadcast_to(second[b][s : s + 1, :], (SUB, BATCH)) * (1.0 / diag)
        second_scaled = second_row * inv_root
        for i in range(b, blocks):
            column = jnp.broadcast_to(work[i][:, j : j + 1], (SUB, BATCH))
            if i == b:
                below = sub > s
                column = jnp.where(below, column, 0.0)
                cleared = jnp.where(jnp.logical_and(at_lane, below), 0.0, work[i])
                work[i] = cleared - column * scaled
                second[i] = jnp.where(sub == s, second_row, second[i] - column * second_scaled)
            else:
                work[i] = jnp.where(at_lane, 0.0, work[i]) - column * scaled
                second[i] = second[i] - column * second_scaled
        scales.append(inv_root)
    firsts = []
    for i in range(blocks):
        scale = scales[SUB * i]
        for s in range(1, SUB):
            scale = jnp.where(sub == s, scales[SUB * i + s], scale)
        diagonal = lane == sub + SUB * i
        unit = jnp.where(diagonal, 1.0, jnp.where(lane < sub + SUB * i, work[i], 0.0))
        firsts.append(unit * scale)
    return jnp.concatenate(firsts, 0), jnp.concatenate(second, 0)


def filter_kernel(
    state_ref, obs_ref, taper_ref, tile_ref, given_ref, order_ref, out_ref, held, weights, picked_given
):
    nobs = obs_ref.shape[0]
    batches = nobs // BATCH
    tiles_dev = tile_ref.shape[0]
    index = lax.broadcasted_iota(jnp.int32, (BATCH, nobs), 1)
    dot = functools.partial(jnp.dot, preferred_element_type=F32)

    def arrange(num, carry):
        rows = pl.ds(pl.multiple_of(num * BATCH, BATCH), BATCH)
        select = (order_ref[rows, :] == index).astype(F32).astype(BF16)
        value = obs_ref[...]
        high, rest = halves(value)
        low = (value - high.astype(F32) - rest.astype(F32)).astype(BF16)
        held[rows, :] = dot(select, high) + (dot(select, rest) + dot(select, low))
        given = given_ref[...]
        high, rest = halves(given)
        low = (given - high.astype(F32) - rest.astype(F32)).astype(BF16)
        picked_given[rows, :] = dot(select, high) + (dot(select, rest) + dot(select, low))
        weights[rows, :] = dot(select, taper_ref[...].astype(BF16))
        return carry

    lax.fori_loop(0, batches, arrange, 0)
    out_ref[...] = state_ref[...]
    eye = lax.broadcasted_iota(jnp.int32, (BATCH, BATCH), 0) == lax.broadcasted_iota(
        jnp.int32, (BATCH, BATCH), 1
    )

    def batch_step(num, carry):
        rows = pl.ds(pl.multiple_of(num * BATCH, BATCH), BATCH)
        batch_obs = held[rows, :]
        row_mean = jnp.mean(batch_obs, axis=1, keepdims=True)
        perturb = batch_obs - row_mean
        given = picked_given[rows, :]
        innov = given[:, 0:1] - row_mean
        variance = given[:, 1:2]
        root_row = jnp.sum(jnp.where(eye, jnp.sqrt(variance), 0.0), axis=0, keepdims=True)
        split = halves(perturb)
        scaled = halves(perturb * (1.0 / (MEMBERS - 1)))
        covariance = dot3(split, scaled, NT) + jnp.where(eye, variance, 0.0)
        first, second = factor_inverses(covariance, root_row)
        first = halves(first)
        middle = dot3(first, halves(jnp.broadcast_to(innov, (BATCH, MEMBERS)))) - dot3(
            halves(second), split
        )
        change = halves(dot3(first, halves(middle), TN))

        def update(ref, place, weight):
            value = ref[place, :]
            product = dot3(halves(value), scaled, NT) * weight
            ref[place, :] = value + dot3(halves(product), change)

        def update_obs(other, inner):
            place = pl.ds(pl.multiple_of(other * BATCH, BATCH), BATCH)
            update(held, place, weights[place, rows])
            return inner

        lax.fori_loop(num + 1, batches, update_obs, 0)
        for tile in range(tiles_dev):
            update(out_ref, pl.ds(tile * TILE, TILE), tile_ref[tile : tile + 1, rows])
        return carry

    lax.fori_loop(0, batches, batch_step, 0)


def filter_all(state, every_obs, taper, tile_taper, given, order_column):
    nobs = every_obs.shape[0]
    return pl.pallas_call(
        filter_kernel,
        out_shape=jax.ShapeDtypeStruct(state.shape, F32),
        in_specs=[VMEM] * 6,
        out_specs=VMEM,
        scratch_shapes=[
            pltpu.VMEM((nobs, MEMBERS), F32),
            pltpu.VMEM((nobs, nobs), F32),
            pltpu.VMEM((nobs, given.shape[1]), F32),
        ],
        compiler_params=pltpu.CompilerParams(vmem_limit_bytes=48 * 1024 * 1024),
    )(state, every_obs, taper, tile_taper, given, order_column)


def shards(state, foot_tiles, foot_weight, azimuth, obs_value, obs_var, tile_bin, obs_bin, order):
    tiles_dev = state.shape[0] // TILE
    half_tile = TILE // 2
    foot_count = foot_tiles.shape[0]
    row_index = lax.axis_index("rows")
    local_tile = foot_tiles - row_index * tiles_dev
    onehot = (
        local_tile[:, :, None] == jnp.arange(tiles_dev, dtype=jnp.int32)[None, None, :]
    ).astype(F32)
    coefficients = jnp.einsum("ftq,ftc->fqc", onehot, foot_weight, precision=HIGH)
    partial_value = jnp.einsum(
        "fqhc,qhcm->fhm",
        coefficients.reshape(foot_count, tiles_dev, 2, half_tile),
        state.reshape(tiles_dev, 2, half_tile, MEMBERS),
        precision=HIGH,
    )
    sorter = (jnp.arange(order.shape[0], dtype=jnp.int32)[:, None] == order[None, :]).astype(BF16)
    own_taper = jnp.dot(taper_weight(obs_bin).astype(BF16), sorter, preferred_element_type=F32)
    tile_taper = jnp.dot(taper_weight(tile_bin).astype(BF16), sorter, preferred_element_type=F32)
    taper = lax.all_gather(own_taper, "obs", axis=0, tiled=True)
    wind_sums = lax.psum(partial_value, "rows")
    angles = azimuth.reshape(foot_count, 4)
    group_obs = model_function(
        wind_sums[:, 0, None, :], wind_sums[:, 1, None, :], angles[:, :, None]
    ).reshape(foot_count * 4, MEMBERS)
    every_obs = lax.all_gather(group_obs, "obs", axis=0, tiled=True)
    given = jnp.stack([obs_value, obs_var], axis=1)
    return filter_all(state, every_obs, taper, tile_taper, given, order[:, None])


def solution(mesh):
    return jax.shard_map(
        shards,
        mesh=mesh,
        in_specs=(
            P(("obs", "rows"), None),
            P("obs", None),
            P("obs", None, None),
            P("obs"),
            P(),
            P(),
            P(("obs", "rows"), None),
            P("obs", None),
            P(),
        ),
        out_specs=P(("obs", "rows"), None),
        check_vma=False,
    )
```

```python
import functools

import jax
import jax.numpy as jnp
from jax import lax
from jax.experimental import pallas as pl
from jax.experimental.pallas import tpu as pltpu
from jax.sharding import PartitionSpec as P

MEMBERS = 256
BATCH = 128
TILE = 256
RADIUS = 8
SUB = 8
F32 = jnp.float32
BF16 = jnp.bfloat16


HIGH = lax.Precision.HIGHEST
VMEM = pl.BlockSpec(memory_space=pltpu.VMEM)


def model_function(east_wind, north_wind, angles):
    speed = jnp.sqrt(east_wind * east_wind + north_wind * north_wind + 1.0)
    cosine = (east_wind * jnp.cos(angles) + north_wind * jnp.sin(angles)) / speed
    return jnp.exp(0.6 * jnp.log(speed)) * (0.7 + 0.4 * cosine + 0.6 * cosine * cosine)


def taper_weight(bins):
    scaled = 1.0 - bins.astype(F32) / RADIUS
    return jnp.where(bins < RADIUS, scaled * scaled, jnp.zeros_like(scaled))


def halves(value):
    high = value.astype(BF16)
    return high, (value - high.astype(F32)).astype(BF16)


def dot3(left, right, dims=(((1,), (0,)), ((), ()))):
    (left_hi, left_lo), (right_hi, right_lo) = left, right
    dot = functools.partial(lax.dot_general, dimension_numbers=dims, preferred_element_type=F32)
    return dot(left_hi, right_hi) + (dot(left_hi, right_lo) + dot(left_lo, right_hi))


NT = (((1,), (1,)), ((), ()))
TN = (((0,), (0,)), ((), ()))


def factor_inverses(covariance, root_row):
    blocks = BATCH // SUB
    lane = lax.broadcasted_iota(jnp.int32, (SUB, BATCH), 1)
    sub = lax.broadcasted_iota(jnp.int32, (SUB, BATCH), 0)
    work = [covariance[SUB * i : SUB * (i + 1), :] for i in range(blocks)]
    second = [(lane == sub + SUB * i).astype(F32) for i in range(blocks)]

    def across(value, column):
        return jnp.broadcast_to(value[:, column : column + 1], (SUB, BATCH))

    def down(value, row):
        return jnp.broadcast_to(value[row : row + 1, :], (SUB, BATCH))

    for b in range(blocks):
        base = SUB * b
        inside = jnp.logical_and(lane >= base, lane < base + SUB)
        columns = [across(work[b], base + k) for k in range(SUB)]
        solved = jnp.where(inside, (lane == sub + base).astype(F32), work[b])
        forward, own, scale = solved, second[b], jnp.zeros((SUB, BATCH), F32)
        transposed = [jnp.zeros((SUB, BATCH), F32) for _ in range(SUB)]
        for k in range(SUB):
            pivot = down(columns[k], k)
            inv_root = lax.rsqrt(pivot)
            inv = inv_root * inv_root
            other, here = sub != k, sub == k
            for m in range(k + 1, SUB):
                ratio = down(columns[m], k) * inv
                columns[m] = jnp.where(other, columns[m] - columns[k] * ratio, ratio)
                transposed[m] = jnp.where(here, ratio, transposed[m])
            row = down(solved, k) * inv
            solved = jnp.where(other, solved - columns[k] * row, row)
            below = jnp.where(sub > k, columns[k], 0.0)
            forward = forward - below * (down(forward, k) * inv)
            row = down(own, k) * (1.0 / (pivot * inv_root + across(root_row, base + k)))
            own = jnp.where(here, row, own - below * (inv_root * row))
            scale = jnp.where(here, inv_root, scale)
        spread = own * scale
        for m in range(SUB - 1, 0, -1):
            spread = spread - transposed[m] * down(spread, m)
        for i in range(b + 1, blocks):
            panel = [across(work[i], base + k) for k in range(SUB)]
            value, extra = jnp.where(inside, 0.0, work[i]), second[i]
            for k in range(SUB):
                value = value - panel[k] * down(solved, k)
                extra = extra - panel[k] * down(spread, k)
            work[i], second[i] = value, extra
        work[b] = jnp.where(lane <= sub + base, forward * scale, 0.0)
        second[b] = own
    return jnp.concatenate(work, 0), jnp.concatenate(second, 0)


def filter_kernel(
    state_ref, obs_ref, taper_ref, tile_ref, given_ref, order_ref, out_ref, held, weights, picked_given
):
    nobs = obs_ref.shape[0]
    batches = nobs // BATCH
    tiles_dev = tile_ref.shape[0]
    index = lax.broadcasted_iota(jnp.int32, (BATCH, nobs), 1)
    dot = functools.partial(jnp.dot, preferred_element_type=F32)

    def arrange(num, carry):
        rows = pl.ds(pl.multiple_of(num * BATCH, BATCH), BATCH)
        select = (order_ref[rows, :] == index).astype(F32).astype(BF16)
        value = obs_ref[...]
        high, rest = halves(value)
        low = (value - high.astype(F32) - rest.astype(F32)).astype(BF16)
        held[rows, :] = dot(select, high) + (dot(select, rest) + dot(select, low))
        given = given_ref[...]
        high, rest = halves(given)
        low = (given - high.astype(F32) - rest.astype(F32)).astype(BF16)
        picked_given[rows, :] = dot(select, high) + (dot(select, rest) + dot(select, low))
        weights[rows, :] = dot(select, taper_ref[...].astype(BF16))
        return carry

    lax.fori_loop(0, batches, arrange, 0)
    out_ref[...] = state_ref[...]
    eye = lax.broadcasted_iota(jnp.int32, (BATCH, BATCH), 0) == lax.broadcasted_iota(
        jnp.int32, (BATCH, BATCH), 1
    )

    def batch_step(num, carry):
        rows = pl.ds(pl.multiple_of(num * BATCH, BATCH), BATCH)
        batch_obs = held[rows, :]
        row_mean = jnp.mean(batch_obs, axis=1, keepdims=True)
        perturb = batch_obs - row_mean
        given = picked_given[rows, :]
        innov = given[:, 0:1] - row_mean
        variance = given[:, 1:2]
        root_row = jnp.sum(jnp.where(eye, jnp.sqrt(variance), 0.0), axis=0, keepdims=True)
        split = halves(perturb)
        scaled = halves(perturb * (1.0 / (MEMBERS - 1)))
        covariance = dot3(split, scaled, NT) + jnp.where(eye, variance, 0.0)
        first, second = factor_inverses(covariance, root_row)
        first = halves(first)
        middle = dot3(first, halves(jnp.broadcast_to(innov, (BATCH, MEMBERS)))) - dot3(
            halves(second), split
        )
        change = halves(dot3(first, halves(middle), TN))

        def update(ref, place, weight):
            value = ref[place, :]
            product = dot3(halves(value), scaled, NT) * weight
            ref[place, :] = value + dot3(halves(product), change)

        def update_obs(other, inner):
            place = pl.ds(pl.multiple_of(other * BATCH, BATCH), BATCH)
            update(held, place, weights[place, rows])
            return inner

        lax.fori_loop(num + 1, batches, update_obs, 0)
        for tile in range(tiles_dev):
            update(out_ref, pl.ds(tile * TILE, TILE), tile_ref[tile : tile + 1, rows])
        return carry

    lax.fori_loop(0, batches, batch_step, 0)


def filter_all(state, every_obs, taper, tile_taper, given, order_column):
    nobs = every_obs.shape[0]
    return pl.pallas_call(
        filter_kernel,
        out_shape=jax.ShapeDtypeStruct(state.shape, F32),
        in_specs=[VMEM] * 6,
        out_specs=VMEM,
        scratch_shapes=[
            pltpu.VMEM((nobs, MEMBERS), F32),
            pltpu.VMEM((nobs, nobs), F32),
            pltpu.VMEM((nobs, given.shape[1]), F32),
        ],
        compiler_params=pltpu.CompilerParams(vmem_limit_bytes=48 * 1024 * 1024),
    )(state, every_obs, taper, tile_taper, given, order_column)


def shards(state, foot_tiles, foot_weight, azimuth, obs_value, obs_var, tile_bin, obs_bin, order):
    tiles_dev = state.shape[0] // TILE
    half_tile = TILE // 2
    foot_count = foot_tiles.shape[0]
    row_index = lax.axis_index("rows")
    local_tile = foot_tiles - row_index * tiles_dev
    onehot = (
        local_tile[:, :, None] == jnp.arange(tiles_dev, dtype=jnp.int32)[None, None, :]
    ).astype(F32)
    coefficients = jnp.einsum("ftq,ftc->fqc", onehot, foot_weight, precision=HIGH)
    partial_value = jnp.einsum(
        "fqhc,qhcm->fhm",
        coefficients.reshape(foot_count, tiles_dev, 2, half_tile),
        state.reshape(tiles_dev, 2, half_tile, MEMBERS),
        precision=HIGH,
    )
    sorter = (jnp.arange(order.shape[0], dtype=jnp.int32)[:, None] == order[None, :]).astype(BF16)
    own_taper = jnp.dot(taper_weight(obs_bin).astype(BF16), sorter, preferred_element_type=F32)
    tile_taper = jnp.dot(taper_weight(tile_bin).astype(BF16), sorter, preferred_element_type=F32)
    taper = lax.all_gather(own_taper, "obs", axis=0, tiled=True)
    wind_sums = lax.psum(partial_value, "rows")
    angles = azimuth.reshape(foot_count, 4)
    group_obs = model_function(
        wind_sums[:, 0, None, :], wind_sums[:, 1, None, :], angles[:, :, None]
    ).reshape(foot_count * 4, MEMBERS)
    every_obs = lax.all_gather(group_obs, "obs", axis=0, tiled=True)
    given = jnp.stack([obs_value, obs_var], axis=1)
    return filter_all(state, every_obs, taper, tile_taper, given, order[:, None])


def solution(mesh):
    return jax.shard_map(
        shards,
        mesh=mesh,
        in_specs=(
            P(("obs", "rows"), None),
            P("obs", None),
            P("obs", None, None),
            P("obs"),
            P(),
            P(),
            P(("obs", "rows"), None),
            P("obs", None),
            P(),
        ),
        out_specs=P(("obs", "rows"), None),
        check_vma=False,
    )
```

```python
import functools

import jax
import jax.numpy as jnp
from jax import lax
from jax.experimental import pallas as pl
from jax.experimental.pallas import tpu as pltpu
from jax.sharding import PartitionSpec as P

MEMBERS = 256
BATCH = 128
TILE = 256
RADIUS = 8
SUB = 8
F32 = jnp.float32
BF16 = jnp.bfloat16


HIGH = lax.Precision.HIGHEST
MESH = pl.DeviceIdType.MESH
VMEM = pl.BlockSpec(memory_space=pltpu.VMEM)


def model_function(east_wind, north_wind, cosines, sines):
    speed = jnp.sqrt(east_wind * east_wind + north_wind * north_wind + 1.0)
    cosine = (east_wind * cosines + north_wind * sines) / speed
    return jnp.exp(0.6 * jnp.log(speed)) * (0.7 + 0.4 * cosine + 0.6 * cosine * cosine)


def taper_weight(bins):
    scaled = 1.0 - bins.astype(F32) / RADIUS
    return jnp.where(bins < RADIUS, scaled * scaled, jnp.zeros_like(scaled))


def halves(value):
    high = value.astype(BF16)
    return high, (value - high.astype(F32)).astype(BF16)


def dot3(left, right, dims=(((1,), (0,)), ((), ()))):
    (left_hi, left_lo), (right_hi, right_lo) = left, right
    dot = functools.partial(lax.dot_general, dimension_numbers=dims, preferred_element_type=F32)
    return dot(left_hi, right_hi) + (dot(left_hi, right_lo) + dot(left_lo, right_hi))


NT = (((1,), (1,)), ((), ()))
TN = (((0,), (0,)), ((), ()))


def factor_inverses(covariance, root_row):
    blocks = BATCH // SUB
    lane = lax.broadcasted_iota(jnp.int32, (SUB, BATCH), 1)
    sub = lax.broadcasted_iota(jnp.int32, (SUB, BATCH), 0)
    work = [covariance[SUB * i : SUB * (i + 1), :] for i in range(blocks)]
    second = [(lane == sub + SUB * i).astype(F32) for i in range(blocks)]

    def across(value, column):
        return jnp.broadcast_to(value[:, column : column + 1], (SUB, BATCH))

    def down(value, row):
        return jnp.broadcast_to(value[row : row + 1, :], (SUB, BATCH))

    for b in range(blocks):
        base = SUB * b
        inside = jnp.logical_and(lane >= base, lane < base + SUB)
        columns = [across(work[b], base + k) for k in range(SUB)]
        solved = jnp.where(inside, (lane == sub + base).astype(F32), work[b])
        forward, own, scale = solved, second[b], jnp.zeros((SUB, BATCH), F32)
        transposed = [jnp.zeros((SUB, BATCH), F32) for _ in range(SUB)]
        for k in range(SUB):
            pivot = down(columns[k], k)
            inv_root = lax.rsqrt(pivot)
            inv = inv_root * inv_root
            other, here = sub != k, sub == k
            for m in range(k + 1, SUB):
                ratio = down(columns[m], k) * inv
                columns[m] = jnp.where(other, columns[m] - columns[k] * ratio, ratio)
                transposed[m] = jnp.where(here, ratio, transposed[m])
            row = down(solved, k) * inv
            solved = jnp.where(other, solved - columns[k] * row, row)
            below = jnp.where(sub > k, columns[k], 0.0)
            forward = forward - below * (down(forward, k) * inv)
            row = down(own, k) * (1.0 / (pivot * inv_root + across(root_row, base + k)))
            own = jnp.where(here, row, own - below * (inv_root * row))
            scale = jnp.where(here, inv_root, scale)
        spread = own * scale
        for m in range(SUB - 1, 0, -1):
            spread = spread - transposed[m] * down(spread, m)
        for i in range(b + 1, blocks):
            panel = [across(work[i], base + k) for k in range(SUB)]
            value, extra = jnp.where(inside, 0.0, work[i]), second[i]
            for k in range(SUB):
                value = value - panel[k] * down(solved, k)
                extra = extra - panel[k] * down(spread, k)
            work[i], second[i] = value, extra
        work[b] = jnp.where(lane <= sub + base, forward * scale, 0.0)
        second[b] = own
    return jnp.concatenate(work, 0), jnp.concatenate(second, 0)


def filter_kernel(
    group_size, state_ref, obs_ref, taper_ref, tile_ref, given_ref, order_ref, order_row_ref, out_ref, held, weights, picked_given
):
    nobs = obs_ref.shape[0]
    batches = nobs // BATCH
    tiles_dev = tile_ref.shape[0]
    index = lax.broadcasted_iota(jnp.int32, (BATCH, nobs), 1)
    dot = functools.partial(jnp.dot, preferred_element_type=F32)

    lane = lax.broadcasted_iota(jnp.int32, (BATCH, BATCH), 1)
    before = lane < lax.broadcasted_iota(jnp.int32, (BATCH, BATCH), 0)

    def pick(select, value):
        high, rest = halves(value)
        low = (value - high.astype(F32) - rest.astype(F32)).astype(BF16)
        return dot(select, high) + (dot(select, rest) + dot(select, low))

    def arrange(num, carry):
        rows = pl.ds(pl.multiple_of(num * BATCH, BATCH), BATCH)
        wanted = order_ref[rows, :]
        select = (wanted == index).astype(F32).astype(BF16)
        picked_given[rows, :] = pick(select, given_ref[...])
        group = wanted // group_size
        same = jnp.logical_and(before, group == order_row_ref[:, rows] // group_size)
        earlier = jnp.sum(same.astype(F32), axis=1, keepdims=True).astype(jnp.int32)
        place = group * (group_size // batches) + earlier
        select = (place == lane).astype(F32).astype(BF16)
        held[rows, :] = pick(select, obs_ref[rows, :])
        weights[rows, :] = dot(select, taper_ref[rows, :].astype(BF16))
        return carry

    lax.fori_loop(0, batches, arrange, 0)
    out_ref[...] = state_ref[...]
    eye = lax.broadcasted_iota(jnp.int32, (BATCH, BATCH), 0) == lax.broadcasted_iota(
        jnp.int32, (BATCH, BATCH), 1
    )

    def batch_step(num, carry):
        rows = pl.ds(pl.multiple_of(num * BATCH, BATCH), BATCH)
        batch_obs = held[rows, :]
        row_mean = jnp.mean(batch_obs, axis=1, keepdims=True)
        perturb = batch_obs - row_mean
        given = picked_given[rows, :]
        innov = given[:, 0:1] - row_mean
        variance = given[:, 1:2]
        root_row = jnp.sum(jnp.where(eye, jnp.sqrt(variance), 0.0), axis=0, keepdims=True)
        split = halves(perturb)
        scaled = halves(perturb * (1.0 / (MEMBERS - 1)))
        covariance = dot3(split, scaled, NT) + jnp.where(eye, variance, 0.0)
        first, second = factor_inverses(covariance, root_row)
        first = halves(first)
        middle = dot3(first, halves(jnp.broadcast_to(innov, (BATCH, MEMBERS)))) - dot3(
            halves(second), split
        )
        change = halves(dot3(first, halves(middle), TN))

        def update(ref, place, weight):
            value = ref[place, :]
            product = dot3(halves(value), scaled, NT) * weight
            ref[place, :] = value + dot3(halves(product), change)

        def update_obs(other, inner):
            place = pl.ds(pl.multiple_of(other * BATCH, BATCH), BATCH)
            update(held, place, weights[place, rows])
            return inner

        lax.fori_loop(num + 1, batches, update_obs, 0)
        for tile in range(tiles_dev):
            update(out_ref, pl.ds(tile * TILE, TILE), tile_ref[tile : tile + 1, rows])
        return carry

    lax.fori_loop(0, batches, batch_step, 0)


def filter_all(state, every_obs, taper, tile_taper, given, order, group_size):
    nobs = every_obs.shape[0]
    return pl.pallas_call(
        functools.partial(filter_kernel, group_size),
        out_shape=jax.ShapeDtypeStruct(state.shape, F32),
        in_specs=[VMEM] * 7,
        out_specs=VMEM,
        scratch_shapes=[
            pltpu.VMEM((nobs, MEMBERS), F32),
            pltpu.VMEM((nobs, nobs), F32),
            pltpu.VMEM((nobs, given.shape[1]), F32),
        ],
        compiler_params=pltpu.CompilerParams(vmem_limit_bytes=48 * 1024 * 1024),
    )(state, every_obs, taper, tile_taper, given, order[:, None], order[None, :])


def exchange_kernel(
    groups, layers, state_ref, tiles_ref, weight_ref, cos_ref, sin_ref, order_ref, bins_ref, tile_bin_ref,
    obs_out, taper_out, tile_out, own_sums, sums, own_obs, own_taper,
    sum_send, sum_recv, obs_send, obs_recv, taper_send, taper_recv,
):
    me, layer = lax.axis_index("obs"), lax.axis_index("rows")
    feet, batches, per = tiles_ref.shape[0], own_obs.shape[0], own_obs.shape[1]
    count, nobs = bins_ref.shape
    tiles_dev, half = tile_bin_ref.shape[0], TILE // 2
    barrier = pltpu.get_barrier_semaphore()
    for k in range(1, groups):
        pl.semaphore_signal(barrier, inc=1, device_id={"obs": lax.rem(me + k, groups)}, device_id_type=MESH)
    for k in range(1, layers):
        pl.semaphore_signal(barrier, inc=1, device_id={"rows": lax.rem(layer + k, layers)}, device_id_type=MESH)

    partial = [jnp.zeros((feet, MEMBERS), F32) for _ in range(2)]
    for tile in range(tiles_dev):
        number = layer * tiles_dev + tile
        factor = jnp.zeros((feet, TILE), F32)
        for t in range(tiles_ref.shape[1]):
            factor = factor + jnp.where(tiles_ref[:, t : t + 1] == number, weight_ref[:, t, :], 0.0)
        for h in range(2):
            partial[h] = partial[h] + jnp.dot(
                factor[:, h * half : (h + 1) * half],
                state_ref[pl.ds(tile * TILE + h * half, half), :],
                precision=HIGH,
                preferred_element_type=F32,
            )
    for h in range(2):
        own_sums[h] = partial[h]
    pl.semaphore_wait(barrier, groups + layers - 2)

    sum_copies = []
    for k in range(1, layers):
        copy = pltpu.make_async_remote_copy(
            own_sums, sums.at[k], sum_send.at[k], sum_recv.at[k],
            device_id={"rows": lax.rem(layer + k, layers)}, device_id_type=MESH,
        )
        copy.start()
        sum_copies.append(copy)

    order = order_ref[...]
    base = me * count
    steps = lax.broadcasted_iota(jnp.int32, (count, nobs), 1).astype(F32)
    member = jnp.logical_and(order >= base, order < base + count).astype(F32)
    local = lax.broadcasted_iota(jnp.int32, (count, 1), 0)
    column = lax.broadcasted_iota(jnp.int32, (count, count), 1)

    def ranks(ids):
        at = jnp.sum(jnp.where(order == base + ids, steps, 0.0), axis=1, keepdims=True)
        rank = jnp.sum(jnp.where(steps < at, member, 0.0), axis=1, keepdims=True)
        return (rank.astype(jnp.int32) == column).astype(F32)

    sorter = (lax.broadcasted_iota(jnp.int32, (nobs, nobs), 0) == order).astype(F32).astype(BF16)
    ordered = jnp.dot(taper_weight(bins_ref[...]).astype(BF16), sorter, preferred_element_type=F32)
    ordered = lax.dot_general(
        ranks(local).astype(BF16), ordered.astype(BF16), TN, preferred_element_type=F32
    )
    for b in range(batches):
        own_taper[b] = ordered[b * per : (b + 1) * per, :]
        taper_out[b, me] = ordered[b * per : (b + 1) * per, :]
    cuts = [(1, 2), (3, batches - 3)]
    taper_copies = []
    for k in range(1, groups):
        for c, (first, length) in enumerate(cuts):
            wide = pl.ds(0, (first + length - 1) * BATCH)
            copy = pltpu.make_async_remote_copy(
                own_taper.at[pl.ds(first, length), :, wide],
                taper_out.at[pl.ds(first, length), me, :, wide],
                taper_send.at[k, c], taper_recv.at[k, c],
                device_id={"obs": lax.rem(me + k, groups)}, device_id_type=MESH,
            )
            copy.start()
            taper_copies.append(copy)

    tile_out[...] = jnp.dot(taper_weight(tile_bin_ref[...]).astype(BF16), sorter, preferred_element_type=F32)
    chooser = ranks(local % feet * 4 + local // feet)
    for copy in sum_copies:
        copy.wait()
    winds = [own_sums[h] for h in range(2)]
    for k in range(1, layers):
        winds = [winds[h] + sums[k, h] for h in range(2)]
    observed = jnp.concatenate(
        [
            model_function(winds[0], winds[1], cos_ref[:, k : k + 1], sin_ref[:, k : k + 1])
            for k in range(cos_ref.shape[1])
        ],
        0,
    )
    observed = lax.dot_general(chooser, observed, TN, precision=HIGH, preferred_element_type=F32)
    for b in range(batches):
        own_obs[b] = observed[b * per : (b + 1) * per, :]
        obs_out[b, me] = observed[b * per : (b + 1) * per, :]
    obs_copies = []
    for k in range(1, groups):
        copy = pltpu.make_async_remote_copy(
            own_obs, obs_out.at[:, me], obs_send.at[k], obs_recv.at[k],
            device_id={"obs": lax.rem(me + k, groups)}, device_id_type=MESH,
        )
        copy.start()
        obs_copies.append(copy)
    for copy in taper_copies + obs_copies:
        copy.wait()


def exchange(state, foot_tiles, foot_weight, cosines, sines, order_row, obs_bin, tile_bin):
    groups, layers = lax.axis_size("obs"), lax.axis_size("rows")
    count, nobs = obs_bin.shape
    batches, feet = nobs // BATCH, foot_tiles.shape[0]
    per = count // batches
    dma = pltpu.SemaphoreType.DMA
    return pl.pallas_call(
        functools.partial(exchange_kernel, groups, layers),
        out_shape=(
            jax.ShapeDtypeStruct((batches, groups, per, MEMBERS), F32),
            jax.ShapeDtypeStruct((batches, groups, per, nobs), F32),
            jax.ShapeDtypeStruct(tile_bin.shape, F32),
        ),
        in_specs=[VMEM] * 8,
        out_specs=(VMEM, VMEM, VMEM),
        scratch_shapes=[
            pltpu.VMEM((2, feet, MEMBERS), F32),
            pltpu.VMEM((layers, 2, feet, MEMBERS), F32),
            pltpu.VMEM((batches, per, MEMBERS), F32),
            pltpu.VMEM((batches, per, nobs), F32),
            dma((layers,)), dma((layers,)), dma((groups,)), dma((groups,)), dma((groups, 2)), dma((groups, 2)),
        ],
        compiler_params=pltpu.CompilerParams(
            collective_id=0, has_side_effects=True, vmem_limit_bytes=48 * 1024 * 1024
        ),
    )(state, foot_tiles, foot_weight, cosines, sines, order_row, obs_bin, tile_bin)


def shards(state, foot_tiles, foot_weight, azimuth, obs_value, obs_var, tile_bin, obs_bin, order):
    angles = azimuth.reshape(foot_tiles.shape[0], -1)
    every_obs, taper, tile_taper = exchange(
        state, foot_tiles, foot_weight, jnp.cos(angles), jnp.sin(angles), order[None, :], obs_bin, tile_bin
    )
    nobs = order.shape[0]
    given = jnp.stack([obs_value, obs_var], axis=1)
    return filter_all(
        state, every_obs.reshape(nobs, MEMBERS), taper.reshape(nobs, nobs), tile_taper, given, order, obs_bin.shape[0]
    )


def solution(mesh):
    return jax.shard_map(
        shards,
        mesh=mesh,
        in_specs=(
            P(("obs", "rows"), None),
            P("obs", None),
            P("obs", None, None),
            P("obs"),
            P(),
            P(),
            P(("obs", "rows"), None),
            P("obs", None),
            P(),
        ),
        out_specs=P(("obs", "rows"), None),
        check_vma=False,
    )
```

```python
import functools

import jax
import jax.numpy as jnp
from jax import lax
from jax.experimental import pallas as pl
from jax.experimental.pallas import tpu as pltpu
from jax.sharding import PartitionSpec as P

MEMBERS = 256
BATCH = 128
TILE = 256
RADIUS = 8
SUB = 8
F32 = jnp.float32
BF16 = jnp.bfloat16


HIGH = lax.Precision.HIGHEST
MESH = pl.DeviceIdType.MESH
VMEM = pl.BlockSpec(memory_space=pltpu.VMEM)


def model_function(east_wind, north_wind, cosines, sines):
    speed = jnp.sqrt(east_wind * east_wind + north_wind * north_wind + 1.0)
    cosine = (east_wind * cosines + north_wind * sines) / speed
    return jnp.exp(0.6 * jnp.log(speed)) * (0.7 + 0.4 * cosine + 0.6 * cosine * cosine)


def taper_weight(bins):
    scaled = 1.0 - bins.astype(F32) / RADIUS
    return jnp.where(bins < RADIUS, scaled * scaled, jnp.zeros_like(scaled))


def halves(value):
    high = value.astype(BF16)
    return high, (value - high.astype(F32)).astype(BF16)


def dot3(left, right, dims=(((1,), (0,)), ((), ()))):
    (left_hi, left_lo), (right_hi, right_lo) = left, right
    dot = functools.partial(lax.dot_general, dimension_numbers=dims, preferred_element_type=F32)
    return dot(left_hi, right_hi) + (dot(left_hi, right_lo) + dot(left_lo, right_hi))


NT = (((1,), (1,)), ((), ()))
TN = (((0,), (0,)), ((), ()))


def factor_inverses(covariance, root_row):
    blocks = BATCH // SUB
    lane = lax.broadcasted_iota(jnp.int32, (SUB, BATCH), 1)
    sub = lax.broadcasted_iota(jnp.int32, (SUB, BATCH), 0)
    work = [covariance[SUB * i : SUB * (i + 1), :] for i in range(blocks)]
    second = [(lane == sub + SUB * i).astype(F32) for i in range(blocks)]

    def across(value, column):
        return jnp.broadcast_to(value[:, column : column + 1], (SUB, BATCH))

    def down(value, row):
        return jnp.broadcast_to(value[row : row + 1, :], (SUB, BATCH))

    for b in range(blocks):
        base = SUB * b
        inside = jnp.logical_and(lane >= base, lane < base + SUB)
        columns = [across(work[b], base + k) for k in range(SUB)]
        solved = jnp.where(inside, (lane == sub + base).astype(F32), work[b])
        forward, own, scale = solved, second[b], jnp.zeros((SUB, BATCH), F32)
        transposed = [jnp.zeros((SUB, BATCH), F32) for _ in range(SUB)]
        for k in range(SUB):
            pivot = down(columns[k], k)
            inv_root = lax.rsqrt(pivot)
            inv = inv_root * inv_root
            other, here = sub != k, sub == k
            for m in range(k + 1, SUB):
                ratio = down(columns[m], k) * inv
                columns[m] = jnp.where(other, columns[m] - columns[k] * ratio, ratio)
                transposed[m] = jnp.where(here, ratio, transposed[m])
            row = down(solved, k) * inv
            solved = jnp.where(other, solved - columns[k] * row, row)
            below = jnp.where(sub > k, columns[k], 0.0)
            forward = forward - below * (down(forward, k) * inv)
            row = down(own, k) * (1.0 / (pivot * inv_root + across(root_row, base + k)))
            own = jnp.where(here, row, own - below * (inv_root * row))
            scale = jnp.where(here, inv_root, scale)
        spread = own * scale
        for m in range(SUB - 1, 0, -1):
            spread = spread - transposed[m] * down(spread, m)
        for i in range(b + 1, blocks):
            panel = [across(work[i], base + k) for k in range(SUB)]
            value, extra = jnp.where(inside, 0.0, work[i]), second[i]
            for k in range(SUB):
                value = value - panel[k] * down(solved, k)
                extra = extra - panel[k] * down(spread, k)
            work[i], second[i] = value, extra
        work[b] = jnp.where(lane <= sub + base, forward * scale, 0.0)
        second[b] = own
    return jnp.concatenate(work, 0), jnp.concatenate(second, 0)


def filter_kernel(
    group_size, state_ref, obs_ref, taper_ref, tile_ref, given_ref, order_ref, order_row_ref, out_ref, held, weights, picked_given
):
    nobs = obs_ref.shape[0]
    batches = nobs // BATCH
    tiles_dev = tile_ref.shape[0]
    index = lax.broadcasted_iota(jnp.int32, (BATCH, nobs), 1)
    dot = functools.partial(jnp.dot, preferred_element_type=F32)

    lane = lax.broadcasted_iota(jnp.int32, (BATCH, BATCH), 1)
    before = lane < lax.broadcasted_iota(jnp.int32, (BATCH, BATCH), 0)

    def pick(select, value):
        high, rest = halves(value)
        low = (value - high.astype(F32) - rest.astype(F32)).astype(BF16)
        return dot(select, high) + (dot(select, rest) + dot(select, low))

    def arrange(num, carry):
        rows = pl.ds(pl.multiple_of(num * BATCH, BATCH), BATCH)
        wanted = order_ref[rows, :]
        select = (wanted == index).astype(F32).astype(BF16)
        picked_given[rows, :] = pick(select, given_ref[...])
        group = wanted // group_size
        same = jnp.logical_and(before, group == order_row_ref[:, rows] // group_size)
        earlier = jnp.sum(same.astype(F32), axis=1, keepdims=True).astype(jnp.int32)
        place = group * (group_size // batches) + earlier
        select = (place == lane).astype(F32).astype(BF16)
        held[rows, :] = pick(select, obs_ref[rows, :])
        weights[rows, :] = dot(select, taper_ref[rows, :].astype(BF16))
        return carry

    lax.fori_loop(0, batches, arrange, 0)
    out_ref[...] = state_ref[...]
    eye = lax.broadcasted_iota(jnp.int32, (BATCH, BATCH), 0) == lax.broadcasted_iota(
        jnp.int32, (BATCH, BATCH), 1
    )

    def batch_step(num, carry):
        rows = pl.ds(pl.multiple_of(num * BATCH, BATCH), BATCH)
        batch_obs = held[rows, :]
        row_mean = jnp.mean(batch_obs, axis=1, keepdims=True)
        perturb = batch_obs - row_mean
        given = picked_given[rows, :]
        innov = given[:, 0:1] - row_mean
        variance = given[:, 1:2]
        root_row = jnp.sum(jnp.where(eye, jnp.sqrt(variance), 0.0), axis=0, keepdims=True)
        split = halves(perturb)
        scaled = halves(perturb * (1.0 / (MEMBERS - 1)))
        covariance = dot3(split, scaled, NT) + jnp.where(eye, variance, 0.0)
        first, second = factor_inverses(covariance, root_row)
        first = halves(first)
        middle = dot3(first, halves(jnp.broadcast_to(innov, (BATCH, MEMBERS)))) - dot3(
            halves(second), split
        )
        change = halves(dot3(first, halves(middle), TN))

        def update(ref, place, weight):
            value = ref[place, :]
            product = dot3(halves(value), scaled, NT) * weight
            ref[place, :] = value + dot3(halves(product), change)

        def update_obs(other, inner):
            place = pl.ds(pl.multiple_of(other * BATCH, BATCH), BATCH)
            update(held, place, weights[place, rows])
            return inner

        lax.fori_loop(num + 1, batches, update_obs, 0)
        for tile in range(tiles_dev):
            update(out_ref, pl.ds(tile * TILE, TILE), tile_ref[tile : tile + 1, rows])
        return carry

    lax.fori_loop(0, batches, batch_step, 0)


def filter_all(state, every_obs, taper, tile_taper, given, order, group_size):
    nobs = every_obs.shape[0]
    return pl.pallas_call(
        functools.partial(filter_kernel, group_size),
        out_shape=jax.ShapeDtypeStruct(state.shape, F32),
        in_specs=[VMEM] * 7,
        out_specs=VMEM,
        scratch_shapes=[
            pltpu.VMEM((nobs, MEMBERS), F32),
            pltpu.VMEM((nobs, nobs), F32),
            pltpu.VMEM((nobs, given.shape[1]), F32),
        ],
        compiler_params=pltpu.CompilerParams(vmem_limit_bytes=48 * 1024 * 1024),
    )(state, every_obs, taper, tile_taper, given, order[:, None], order[None, :])


def exchange_kernel(
    groups, layers, state_ref, tiles_ref, weight_ref, cos_ref, sin_ref, order_ref, bins_ref, tile_bin_ref,
    obs_out, taper_out, tile_out, own_sums, sums, own_obs, own_taper,
    sum_send, sum_recv, obs_send, obs_recv, taper_send, taper_recv,
):
    me, layer = lax.axis_index("obs"), lax.axis_index("rows")
    feet, batches, per = tiles_ref.shape[0], own_obs.shape[0], own_obs.shape[1]
    count, nobs = bins_ref.shape
    tiles_dev, half = tile_bin_ref.shape[0], TILE // 2
    barrier = pltpu.get_barrier_semaphore()
    for k in range(1, groups):
        pl.semaphore_signal(barrier, inc=1, device_id={"obs": lax.rem(me + k, groups)}, device_id_type=MESH)
    for k in range(1, layers):
        pl.semaphore_signal(barrier, inc=1, device_id={"rows": lax.rem(layer + k, layers)}, device_id_type=MESH)

    partial = [jnp.zeros((feet, MEMBERS), F32) for _ in range(2)]
    for tile in range(tiles_dev):
        number = layer * tiles_dev + tile
        factor = jnp.zeros((feet, TILE), F32)
        for t in range(tiles_ref.shape[1]):
            factor = factor + jnp.where(tiles_ref[:, t : t + 1] == number, weight_ref[:, t, :], 0.0)
        for h in range(2):
            partial[h] = partial[h] + jnp.dot(
                factor[:, h * half : (h + 1) * half],
                state_ref[pl.ds(tile * TILE + h * half, half), :],
                precision=HIGH,
                preferred_element_type=F32,
            )
    for h in range(2):
        own_sums[h] = partial[h]
    pl.semaphore_wait(barrier, groups + layers - 2)

    sum_copies = []
    for k in range(1, layers):
        copy = pltpu.make_async_remote_copy(
            own_sums, sums.at[k], sum_send.at[k], sum_recv.at[k],
            device_id={"rows": lax.rem(layer + k, layers)}, device_id_type=MESH,
        )
        copy.start()
        sum_copies.append(copy)

    order = order_ref[...]
    base = me * count
    steps = lax.broadcasted_iota(jnp.int32, (count, nobs), 1).astype(F32)
    member = jnp.logical_and(order >= base, order < base + count).astype(F32)
    local = lax.broadcasted_iota(jnp.int32, (count, 1), 0)
    column = lax.broadcasted_iota(jnp.int32, (count, count), 1)

    def ranks(ids):
        at = jnp.sum(jnp.where(order == base + ids, steps, 0.0), axis=1, keepdims=True)
        rank = jnp.sum(jnp.where(steps < at, member, 0.0), axis=1, keepdims=True)
        return (rank.astype(jnp.int32) == column).astype(F32)

    sorter = (lax.broadcasted_iota(jnp.int32, (nobs, nobs), 0) == order).astype(F32).astype(BF16)
    ordered = jnp.dot(taper_weight(bins_ref[...]).astype(BF16), sorter, preferred_element_type=F32)
    ordered = lax.dot_general(
        ranks(local).astype(BF16), ordered.astype(BF16), TN, preferred_element_type=F32
    )
    for b in range(batches):
        own_taper[b] = ordered[b * per : (b + 1) * per, :]
        taper_out[b, me] = ordered[b * per : (b + 1) * per, :]
    cuts = [(b, 1) for b in range(1, batches)]
    taper_copies = []
    for k in range(1, groups):
        for c, (first, length) in enumerate(cuts):
            wide = pl.ds(0, (first + length - 1) * BATCH)
            copy = pltpu.make_async_remote_copy(
                own_taper.at[pl.ds(first, length), :, wide],
                taper_out.at[pl.ds(first, length), me, :, wide],
                taper_send.at[k, c], taper_recv.at[k, c],
                device_id={"obs": lax.rem(me + k, groups)}, device_id_type=MESH,
            )
            copy.start()
            taper_copies.append(copy)

    tile_out[...] = jnp.dot(taper_weight(tile_bin_ref[...]).astype(BF16), sorter, preferred_element_type=F32)
    chooser = ranks(local % feet * 4 + local // feet)
    for copy in sum_copies:
        copy.wait()
    winds = [own_sums[h] for h in range(2)]
    for k in range(1, layers):
        winds = [winds[h] + sums[k, h] for h in range(2)]
    observed = jnp.concatenate(
        [
            model_function(winds[0], winds[1], cos_ref[:, k : k + 1], sin_ref[:, k : k + 1])
            for k in range(cos_ref.shape[1])
        ],
        0,
    )
    observed = lax.dot_general(chooser, observed, TN, precision=HIGH, preferred_element_type=F32)
    for b in range(batches):
        own_obs[b] = observed[b * per : (b + 1) * per, :]
        obs_out[b, me] = observed[b * per : (b + 1) * per, :]
    obs_copies = []
    for k in range(1, groups):
        copy = pltpu.make_async_remote_copy(
            own_obs, obs_out.at[:, me], obs_send.at[k], obs_recv.at[k],
            device_id={"obs": lax.rem(me + k, groups)}, device_id_type=MESH,
        )
        copy.start()
        obs_copies.append(copy)
    for copy in taper_copies + obs_copies:
        copy.wait()


def exchange(state, foot_tiles, foot_weight, cosines, sines, order_row, obs_bin, tile_bin):
    groups, layers = lax.axis_size("obs"), lax.axis_size("rows")
    count, nobs = obs_bin.shape
    batches, feet = nobs // BATCH, foot_tiles.shape[0]
    per = count // batches
    dma = pltpu.SemaphoreType.DMA
    return pl.pallas_call(
        functools.partial(exchange_kernel, groups, layers),
        out_shape=(
            jax.ShapeDtypeStruct((batches, groups, per, MEMBERS), F32),
            jax.ShapeDtypeStruct((batches, groups, per, nobs), F32),
            jax.ShapeDtypeStruct(tile_bin.shape, F32),
        ),
        in_specs=[VMEM] * 8,
        out_specs=(VMEM, VMEM, VMEM),
        scratch_shapes=[
            pltpu.VMEM((2, feet, MEMBERS), F32),
            pltpu.VMEM((layers, 2, feet, MEMBERS), F32),
            pltpu.VMEM((batches, per, MEMBERS), F32),
            pltpu.VMEM((batches, per, nobs), F32),
            dma((layers,)), dma((layers,)), dma((groups,)), dma((groups,)), dma((groups, batches)), dma((groups, batches)),
        ],
        compiler_params=pltpu.CompilerParams(
            collective_id=0, has_side_effects=True, vmem_limit_bytes=48 * 1024 * 1024
        ),
    )(state, foot_tiles, foot_weight, cosines, sines, order_row, obs_bin, tile_bin)


def shards(state, foot_tiles, foot_weight, azimuth, obs_value, obs_var, tile_bin, obs_bin, order):
    angles = azimuth.reshape(foot_tiles.shape[0], -1)
    every_obs, taper, tile_taper = exchange(
        state, foot_tiles, foot_weight, jnp.cos(angles), jnp.sin(angles), order[None, :], obs_bin, tile_bin
    )
    nobs = order.shape[0]
    given = jnp.stack([obs_value, obs_var], axis=1)
    return filter_all(
        state, every_obs.reshape(nobs, MEMBERS), taper.reshape(nobs, nobs), tile_taper, given, order, obs_bin.shape[0]
    )


def solution(mesh):
    return jax.shard_map(
        shards,
        mesh=mesh,
        in_specs=(
            P(("obs", "rows"), None),
            P("obs", None),
            P("obs", None, None),
            P("obs"),
            P(),
            P(),
            P(("obs", "rows"), None),
            P("obs", None),
            P(),
        ),
        out_specs=P(("obs", "rows"), None),
        check_vma=False,
    )
```
